512 devices in a mesh: uly: 8 (over z_hi, y), blk: 64 (over z_lo, x, core).
Axes of the slice: x: 4, y: 4, z: 16 (z_hi: 2, z_lo: 8; z = z_hi * 8 + z_lo), core: 2. Of those that a mesh axis runs over, the one named last changes fastest.
Arguments:
- query_tokens: bfloat16 [128, 384, 3072], P('blk', 'uly'), may hold values from -18 to 18
- key_tokens: bfloat16 [128, 384, 3072], P('blk', 'uly'), may hold values from -18 to 18
- value_tokens: bfloat16 [128, 384, 3072], P('blk', 'uly'), may hold values from -6 to 6
- grad_tokens: bfloat16 [128, 384, 3072], P('blk', 'uly'), may hold values from -6 to 6
- tile_pairs: int32 [128, 4], replicated, may hold values from 0 to 127, as said below
Outputs:
- grad_query: bfloat16 [128, 384, 3072], P('blk', 'uly')
- grad_key: bfloat16 [128, 384, 3072], P('blk', 'uly')
- grad_value: bfloat16 [128, 384, 3072], P('blk', 'uly')
The draws below stay inside these ranges and needn't reach their ends.
Inputs may be any that keep to these rules, and one draw needn't show every extreme that they name: tile_pairs[i, 0] = i; each row names 4 different tiles; every kept tile j of row i has |j // 2 - i // 2| <= 1, and that distance is reached.
All inputs are finite; a program needn't handle non-finite values.
Results may differ from the reference program's by a relative error of at most 0.0091.
Values may be sent and summed in bfloat16 or wider, within the bound.
A program may use at most 64 MiB of HBM per device.

```python
import math
import jax
import jax.numpy as jnp
from jax import lax

HD = 128
HEADS = 24
TILE = 384
KEEP = 4
REACH = 1
TILE_DEV = 2
TILES = 128


def drawn_rows(key):
    full_shape = (TILES, TILE, HEADS * HD)
    query_draw = jnp.clip(jax.random.normal(jax.random.fold_in(key, 101), full_shape, jnp.float32), -6.0, 6.0)
    key_draw = jnp.clip(jax.random.normal(jax.random.fold_in(key, 102), full_shape, jnp.float32), -6.0, 6.0)
    return (query_draw, key_draw)


def draw_query_tokens(key, part):
    return drawn_rows(key)[0].astype(jnp.bfloat16)


def draw_key_tokens(key, part):
    return drawn_rows(key)[1].astype(jnp.bfloat16)


def draw_tile_pairs(key, part):
    span = (2 * REACH + 1) * TILE_DEV
    tile_ids = lax.broadcasted_iota(jnp.int32, (TILES, 1), 0)
    column_ids = lax.broadcasted_iota(jnp.int32, (TILES, span), 1)
    candidates = (tile_ids // TILE_DEV - REACH) * TILE_DEV + column_ids
    allowed = (candidates >= 0) & (candidates < TILES) & (candidates != tile_ids)
    scores = jax.random.randint(jax.random.fold_in(key, 7), (TILES, span), 0, 1 << 20, dtype=jnp.int32) * span + column_ids
    forced = (tile_ids == 0) & (column_ids == 2 * REACH * TILE_DEV)
    scores = jnp.where(forced, jnp.int32(2 ** 30), scores)
    scores = jnp.where(allowed, scores, jnp.int32(-1))
    chosen = lax.top_k(scores, KEEP - 1)[1]
    picked = jnp.take_along_axis(candidates, chosen, axis=1)
    return jnp.concatenate([tile_ids, picked], axis=1).astype(jnp.int32)


def level_of(rng, shape, shards, smallest, top_value):
    level = 1.0
    for position, parts in shards:
        draws = jax.random.uniform(jax.random.fold_in(jax.random.fold_in(rng, 6), position), (parts,), jnp.float32, smallest / len(shards), top_value / len(shards))
        level = level * jnp.repeat(jnp.exp(draws), shape[position] // parts).reshape((-1,) + (1,) * (len(shape) - 1 - position))
    return level


def scatter_about(rng, extent, width, reach, shards=(), kind=jnp.bfloat16):
    drawn = width * jax.random.normal(rng, extent, jnp.float32)
    if shards:
        drawn = drawn * level_of(rng, extent, shards, -0.22, 0.18)
    return jnp.clip(drawn, -reach, reach).astype(kind)


def setup_inputs(seed: int = 0) -> dict:
    seeds = jax.random.split(jax.random.key(seed), 6)
    return {
        "query_tokens": draw_query_tokens(jax.random.fold_in(seeds[5], 71), 0),
        "key_tokens": draw_key_tokens(jax.random.fold_in(seeds[5], 71), 0),
        "value_tokens": scatter_about(seeds[2], (TILES, TILE, HEADS * HD), 1.0, 6.0, ((0, 64), (1, 8))),
        "grad_tokens": scatter_about(seeds[3], (TILES, TILE, HEADS * HD), 1.0, 6.0, ((0, 64), (1, 8))),
        "tile_pairs": draw_tile_pairs(jax.random.fold_in(seeds[5], 71), 0),
    }


def round_low(values):
    return lax.optimization_barrier(values.astype(jnp.bfloat16)).astype(jnp.float32)

def reference(query_tokens, key_tokens, value_tokens, grad_tokens, tile_pairs):
    scale = 1.0 / math.sqrt(HD)
    flat_pairs = tile_pairs.reshape(-1)

    def per_head(head_index):
        start = (head_index * HD).astype(jnp.int32)
        query_head = lax.dynamic_slice_in_dim(query_tokens, start, HD, 2).astype(jnp.float32)
        key_head = lax.dynamic_slice_in_dim(key_tokens, start, HD, 2).astype(jnp.float32)
        value_head = lax.dynamic_slice_in_dim(value_tokens, start, HD, 2).astype(jnp.float32)
        grad_head = lax.dynamic_slice_in_dim(grad_tokens, start, HD, 2).astype(jnp.float32)
        key_rows = key_head[tile_pairs].reshape(TILES, KEEP * TILE, HD)
        value_rows = value_head[tile_pairs].reshape(TILES, KEEP * TILE, HD)
        scores = jnp.einsum('tqd,tkd->tqk', query_head, key_rows) * scale
        row_max = lax.optimization_barrier(jnp.max(scores, axis=-1, keepdims=True))
        log_total = row_max + jnp.log(lax.optimization_barrier(jnp.sum(jnp.exp(scores - row_max), axis=-1, keepdims=True)))
        probs = jnp.exp(scores - log_total)
        probs_low = round_low(probs)
        attended = jnp.einsum('tqk,tkd->tqd', probs_low, value_rows)
        row_dot = lax.optimization_barrier(jnp.sum(grad_head * attended, axis=-1, keepdims=True))
        grad_probs = jnp.einsum('tqd,tkd->tqk', grad_head, value_rows)
        grad_scores = round_low(probs * (grad_probs - row_dot))
        grad_q = jnp.einsum('tqk,tkd->tqd', grad_scores, key_rows) * scale
        key_terms = jnp.einsum('tqk,tqd->tkd', grad_scores, query_head) * scale
        value_terms = jnp.einsum('tqk,tqd->tkd', probs_low, grad_head)
        key_terms = key_terms.reshape(TILES * KEEP, TILE, HD)
        value_terms = value_terms.reshape(TILES * KEEP, TILE, HD)
        grad_k = jax.ops.segment_sum(key_terms, flat_pairs, num_segments=TILES)
        grad_v = jax.ops.segment_sum(value_terms, flat_pairs, num_segments=TILES)
        return (grad_q.astype(jnp.bfloat16), grad_k.astype(jnp.bfloat16), grad_v.astype(jnp.bfloat16))
    heads_q, heads_k, heads_v = lax.map(per_head, jnp.arange(HEADS, dtype=jnp.int32))

    def merge_heads(stacked):
        return jnp.transpose(stacked, (1, 2, 0, 3)).reshape(TILES, TILE, HEADS * HD)
    return (merge_heads(heads_q), merge_heads(heads_k), merge_heads(heads_v))
```

```python
import functools
import math

import jax
import jax.numpy as jnp
from jax import lax
from jax.experimental import pallas as pl
from jax.experimental.pallas import tpu as pltpu
from jax.sharding import PartitionSpec as P

HD = 128
MESH = pl.DeviceIdType.MESH
F32 = jnp.float32
BF16 = jnp.bfloat16
SIDES = 2
AHEAD = 2


def dot(a, b, ca, cb):
    return lax.dot_general(a, b, (((ca,), (cb,)), ((), ())), preferred_element_type=F32)


def kernel(cfg, tp, q, k, v, g, oq, ok, ov, qb, gb, kb, vb, st_s, st_r, dqs, dks, dvs, dqo, dqx, dki, dvi, tk, tv,
           rqo, rqx, rk, rst, rdq, rdk, sqo, sqx, sk, sst, sdq, sdk):
    ny, nb, lh, rows, keep = cfg
    half = ny * rows
    width = lh * HD
    scale = 1.0 / math.sqrt(HD)
    u, b = lax.axis_index("uly"), lax.axis_index("blk")
    side, y = u // ny, lax.rem(u, ny)
    other = 1 - side
    has_low, has_high = b > 0, b < nb - 1

    def there(i):
        return lax.rem(y + i, ny)

    def near(delta, action):
        if delta == 0:
            action()
        elif delta < 0:
            pl.when(has_low)(action)
        else:
            pl.when(has_high)(action)

    def cols(head):
        return pl.ds(pl.multiple_of(head * HD, HD), HD)

    def wide(yy):
        return pl.ds(pl.multiple_of(yy * width, HD), width)

    def part(base, yy):
        return pl.ds(pl.multiple_of(base + yy * rows, 16), rows)

    def send(src, dst, ssem, rsem, target):
        pltpu.make_async_remote_copy(
            src_ref=src, dst_ref=dst, send_sem=ssem, recv_sem=rsem, device_id=target, device_id_type=MESH
        ).start()

    def take(ref, sem):
        pltpu.make_async_copy(ref, ref, sem).wait()

    bar = pltpu.get_barrier_semaphore()

    def greet(target):
        pl.semaphore_signal(bar, inc=1, device_id=target, device_id_type=MESH)

    for i in range(ny):
        if i:
            greet((side * ny + there(i), b))
        greet((other * ny + there(i), b))
        near(-1, lambda i=i: greet((side * ny + there(i), b - 1)))
        near(1, lambda i=i: greet((side * ny + there(i), b + 1)))
    pl.semaphore_wait(bar, 2 * ny - 1 + ny * (has_low.astype(jnp.int32) + has_high.astype(jnp.int32)))

    def cross(head):
        for i in range(ny):
            yy = there(i)
            target = (other * ny + yy, b)
            for n, (src, dst) in enumerate(((q, qb), (g, gb))):
                send(
                    src.at[:, :, cols(yy * lh + head)],
                    dst.at[:, part(side * half, y), cols(head)],
                    sqx.at[n], rqx.at[n, head], target,
                )

    cross(0)
    for i in range(ny):
        yy = there(i)
        for n, (src, dst) in enumerate(((q, qb), (g, gb))):
            a, z = src.at[:, :, wide(yy)], dst.at[:, part(side * half, y), :]
            if i == 0:
                pltpu.make_async_copy(a, z, rqo.at[n]).start()
            else:
                send(a, z, sqo.at[n], rqo.at[n], (side * ny + yy, b))
    for delta in (0, 1, -1):

        def spread(delta=delta):
            for i in range(ny):
                yy = there(i)
                for n, (src, dst) in enumerate(((k, kb), (v, vb))):
                    a, z = src.at[:, :, wide(yy)], dst.at[pl.ds(2 * (1 - delta), 2), part(0, y), :]
                    if delta == 0 and i == 0:
                        pltpu.make_async_copy(a, z, rk.at[n, 1]).start()
                    else:
                        send(a, z, sk.at[n, 1 + delta], rk.at[n, 1 - delta], (side * ny + yy, b + delta))

        near(delta, spread)
    for head in range(1, AHEAD):
        cross(head)

    def clear(at):
        dki[at] = jnp.zeros(dki.shape[1:], BF16)
        dvi[at] = jnp.zeros(dvi.shape[1:], BF16)

    pl.when(jnp.logical_not(has_low))(lambda: clear(0))
    pl.when(jnp.logical_not(has_high))(lambda: clear(2))

    for n, buf in enumerate((qb, gb)):
        take(buf.at[:, pl.ds(pl.multiple_of(side * half, 16), half), :], rqo.at[n])
    for delta in (0, 1, -1):

        def arrived(delta=delta):
            for n, buf in enumerate((kb, vb)):
                take(buf.at[pl.ds(2 * (1 + delta), 2)], rk.at[n, 1 + delta])

        near(delta, arrived)

    def slot(t, s):
        return jnp.clip(tp[2 * b + t, s] - 2 * b + 2, 0, 5)

    def merge(l1, r1, l2, r2):
        top = jnp.maximum(l1, l2)
        total = top + jnp.log(jnp.exp(l1 - top) + jnp.exp(l2 - top))
        return total, r1 * jnp.exp(l1 - total) + r2 * jnp.exp(l2 - total)

    def first(head):
        c = cols(head)
        for t in range(2):
            qf, gf = qb[t, :, c], gb[t, :, c]
            log_total = row_dot = None
            for s in range(keep):
                at = slot(t, s)
                scores = dot(kb[at, :, c], qf, 1, 1) * scale
                grad_p = dot(vb[at, :, c], gf, 1, 1)
                top = jnp.max(scores, axis=0, keepdims=True)
                e = jnp.exp(scores - top)
                total = jnp.sum(e, axis=0, keepdims=True)
                weighted = jnp.sum(e * grad_p, axis=0, keepdims=True) / total
                total = top + jnp.log(total)
                if s:
                    log_total, row_dot = merge(log_total, row_dot, total, weighted)
                else:
                    log_total, row_dot = total, weighted
            st_s[head, pl.ds(2 * t, 1), :] = log_total
            st_s[head, pl.ds(2 * t + 1, 1), :] = row_dot
        send(st_s.at[head], st_r.at[head], sst.at[head], rst.at[head], (other * ny + y, b))

    def second(head):
        c = cols(head)
        for t in range(2):
            qf, gf = qb[t, :, c], gb[t, :, c]
            log_total, row_dot = merge(
                st_s[head, pl.ds(2 * t, 1), :], st_s[head, pl.ds(2 * t + 1, 1), :],
                st_r[head, pl.ds(2 * t, 1), :], st_r[head, pl.ds(2 * t + 1, 1), :],
            )
            grad_q = None
            for s in range(keep):
                at = slot(t, s)
                kt = kb[at, :, c]
                probs = jnp.exp(dot(kt, qf, 1, 1) * scale - log_total)
                grad_s = (probs * (dot(vb[at, :, c], gf, 1, 1) - row_dot)).astype(BF16)
                tv[t * keep + s] = dot(probs.astype(BF16), gf, 1, 0)
                tk[t * keep + s] = dot(grad_s, qf, 1, 0)
                term = dot(kt, grad_s, 0, 0)
                grad_q = term if grad_q is None else grad_q + term
            dqs[t, :, c] = (grad_q * scale).T.astype(BF16)
        mine = cols(y * lh + head)
        for i in range(ny):
            yy = there(i)
            send(dqs.at[:, part(other * half, yy), c], dqx.at[:, :, mine], sdq.at[1], rdq.at[1], (other * ny + yy, b))
        for i in range(ny):
            yy = there(i)
            a, z = dqs.at[:, part(side * half, yy), c], dqo.at[:, :, mine]
            if i == 0:
                pltpu.make_async_copy(a, z, rdq.at[0]).start()
            else:
                send(a, z, sdq.at[0], rdq.at[0], (side * ny + yy, b))
        slots = [slot(t, s) for t in range(2) for s in range(keep)]
        for j in range(6):
            for terms, out, factor in ((tk, dks, scale), (tv, dvs, 1.0)):
                total = None
                for n, at in enumerate(slots):
                    term = jnp.where(at == j, terms[n], 0.0)
                    total = term if total is None else total + term
                out[j, :, c] = (total * factor).astype(BF16)
        for delta in (1, -1, 0):

            def back(delta=delta):
                for n, (src, dst) in enumerate(((dks, dki), (dvs, dvi))):
                    for i in range(ny):
                        yy = there(i)
                        a, z = src.at[pl.ds(2 * (1 + delta), 2), part(0, yy), c], dst.at[1 - delta, :, :, mine]
                        if delta == 0 and i == 0:
                            pltpu.make_async_copy(a, z, rdk.at[n, 1]).start()
                        else:
                            send(a, z, sdk.at[n, 1 + delta], rdk.at[n, 1 - delta], (side * ny + yy, b + delta))

            near(delta, back)

    def step(at, carry):
        @pl.when(at < lh)
        def _():
            for n, buf in enumerate((qb, gb)):
                take(buf.at[:, pl.ds(pl.multiple_of(other * half, 16), half), cols(at)], rqx.at[n, at])
            pl.when(at + AHEAD < lh)(lambda: cross(at + AHEAD))
            first(at)

        @pl.when(at >= 1)
        def _():
            take(st_r.at[at - 1], rst.at[at - 1])
            second(at - 1)

        return carry

    lax.fori_loop(0, lh + 1, step, 0)

    most = pl.ds(0, (ny - 1) * width)
    for n, src in enumerate((q, g)):
        take(src.at[:, :, most], sqo.at[n])
        take(src, sqx.at[n])
    for n, src in enumerate((k, v)):
        take(src.at[:, :, most], sk.at[n, 1])
        near(-1, lambda n=n, src=src: take(src, sk.at[n, 0]))
        near(1, lambda n=n, src=src: take(src, sk.at[n, 2]))
    for head in range(lh):
        take(st_s.at[head], sst.at[head])

    for n, (buf, out) in enumerate(((dki, ok), (dvi, ov))):
        take(buf.at[1], rdk.at[n, 1])
        near(-1, lambda n=n, buf=buf: take(buf.at[0], rdk.at[n, 0]))
        near(1, lambda n=n, buf=buf: take(buf.at[2], rdk.at[n, 2]))
        out[...] = (buf[0].astype(F32) + buf[1].astype(F32) + buf[2].astype(F32)).astype(BF16)
        take(buf.at[1, :, :, most], sdk.at[n, 1])
        near(-1, lambda n=n, buf=buf: take(buf.at[0], sdk.at[n, 0]))
        near(1, lambda n=n, buf=buf: take(buf.at[2], sdk.at[n, 2]))
    take(dqo, rdq.at[0])
    take(dqx, rdq.at[1])
    oq[...] = (dqo[...].astype(F32) + dqx[...].astype(F32)).astype(BF16)
    take(dqo.at[:, :, most], sdq.at[0])
    take(dqx, sdq.at[1])


def body(q, k, v, g, tile_pairs):
    ny = lax.axis_size("uly") // SIDES
    nb = lax.axis_size("blk")
    tiles, rows, features = q.shape
    lh = features // HD // ny
    width, half, keep = lh * HD, ny * rows, tile_pairs.shape[1]
    dma = pltpu.SemaphoreType.DMA
    out = jax.ShapeDtypeStruct(q.shape, BF16)
    any_space = pl.BlockSpec(memory_space=pl.ANY)
    vmem = pl.BlockSpec(memory_space=pltpu.VMEM)
    full = pltpu.VMEM((tiles, SIDES * half, width), BF16)
    keys = pltpu.VMEM((3 * tiles, half, width), BF16)
    own = pltpu.VMEM((tiles, rows, features), BF16)
    parts = pltpu.VMEM((3, tiles, rows, features), BF16)
    stats = pltpu.VMEM((lh, 2 * tiles, SIDES * half), F32)
    terms = pltpu.VMEM((tiles * keep, half, HD), F32)
    return pl.pallas_call(
        functools.partial(kernel, (ny, nb, lh, rows, keep)),
        out_shape=(out, out, out),
        in_specs=[pl.BlockSpec(memory_space=pltpu.SMEM)] + [any_space] * 4,
        out_specs=(vmem, vmem, vmem),
        scratch_shapes=[
            full, full, keys, keys, stats, stats, full, keys, keys, own, own, parts, parts, terms, terms,
            dma((2,)), dma((2, lh)), dma((2, 3)), dma((lh,)), dma((2,)), dma((2, 3)),
            dma((2,)), dma((2,)), dma((2, 3)), dma((lh,)), dma((2,)), dma((2, 3)),
        ],
        name="tile_attention_backward",
        compiler_params=pltpu.CompilerParams(collective_id=0, has_side_effects=True, vmem_limit_bytes=50 << 20),
    )(tile_pairs, q, k, v, g)


def solution(mesh):
    split = P("blk", "uly", None)
    return jax.shard_map(
        body, mesh=mesh, in_specs=(split,) * 4 + (P(),), out_specs=(split,) * 3, check_vma=False
    )
```

```python
import functools
import math

import jax
import jax.numpy as jnp
from jax import lax
from jax.experimental import pallas as pl
from jax.experimental.pallas import tpu as pltpu
from jax.sharding import PartitionSpec as P

HD = 128
MESH = pl.DeviceIdType.MESH
F32 = jnp.float32
BF16 = jnp.bfloat16
SIDES = 2
FIRST = 2
AHEAD = 4
LAG = 4
PLANE = 8


def dot(a, b, ca, cb):
    return lax.dot_general(a, b, (((ca,), (cb,)), ((), ())), preferred_element_type=F32)


def kernel(cfg, tp, q, k, v, g, oq, ok, ov, qb, gb, kb, vb, st_s, st_r, dqs, dks, dvs, dkf, dvf, dqo, dqx, dkn, dvn, dko, dvo, tk, tv, pkv, pdkv,
           rqo, rqx, rk, rst, rdq, rdn, rdk, sqo, sqx, sk, sst, sdq, sdn, sdk, rpk, spk, rpd, spd):
    ny, nb, lh, rows, keep = cfg
    half = ny * rows
    width = lh * HD
    scale = 1.0 / math.sqrt(HD)
    u, b = lax.axis_index("uly"), lax.axis_index("blk")
    side, y = u // ny, lax.rem(u, ny)
    other = 1 - side
    has_low, has_high = b > 0, b < nb - 1
    plane, place = b // PLANE, lax.rem(b, PLANE)
    upward = lax.rem(place, 2)
    passed = (place + upward) // 2
    passes = jnp.where(
        upward == 1,
        jnp.logical_and(place < PLANE - 1, plane < nb // PLANE - 1),
        jnp.logical_and(place > 0, plane > 0),
    )
    pass_from = PLANE * plane + (PLANE - 1) * upward
    pass_to = (u, pass_from + 2 * upward - 1)
    pass_in = 1 - upward

    def at_edge(delta):
        return place == (PLANE - 1 if delta > 0 else 0)

    def helper(delta, i):
        return (u, PLANE * plane + (2 * i - 1 if delta > 0 else 2 * i))

    def there(i):
        return lax.rem(y + i, ny)

    def near(delta, action):
        if delta == 0:
            action()
        elif delta < 0:
            pl.when(has_low)(action)
        else:
            pl.when(has_high)(action)

    def cols(head):
        return pl.ds(pl.multiple_of(head * HD, HD), HD)

    def wide(yy):
        return pl.ds(pl.multiple_of(yy * width, HD), width)

    def part(base, yy):
        return pl.ds(pl.multiple_of(base + yy * rows, 16), rows)

    def send(src, dst, ssem, rsem, target):
        pltpu.make_async_remote_copy(
            src_ref=src, dst_ref=dst, send_sem=ssem, recv_sem=rsem, device_id=target, device_id_type=MESH
        ).start()

    def take(ref, sem):
        pltpu.make_async_copy(ref, ref, sem).wait()

    def over(delta, src, dst, ssem, rsem, passing, psem):
        def action():
            @pl.when(at_edge(delta))
            def _():
                for i in range(ny):
                    few = pl.ds(i * rows, rows)
                    if i:
                        send(src(few), passing, ssem, psem, helper(delta, i))
                    else:
                        send(src(few), dst(few), ssem, rsem, (u, b + delta))

            @pl.when(jnp.logical_not(at_edge(delta)))
            def _():
                every = pl.ds(0, half)
                send(src(every), dst(every), ssem, rsem, (u, b + delta))

        near(delta, action)

    bar = pltpu.get_barrier_semaphore()

    def greet(target):
        pl.semaphore_signal(bar, inc=1, device_id=target, device_id_type=MESH)

    for i in range(ny):
        if i:
            greet((side * ny + there(i), b))
        greet((other * ny + there(i), b))

    near(-1, lambda: greet((u, b - 1)))
    near(1, lambda: greet((u, b + 1)))

    def greet_helpers(delta):
        for i in range(1, ny):
            greet(helper(delta, i))
            greet((u, PLANE * (plane + delta) + (2 * i if delta > 0 else 2 * i - 1)))

    def greet_served():
        greet((u, pass_from))
        greet(pass_to)

    up, down = jnp.logical_and(has_high, at_edge(1)), jnp.logical_and(has_low, at_edge(-1))
    pl.when(up)(lambda: greet_helpers(1))
    pl.when(down)(lambda: greet_helpers(-1))
    pl.when(passes)(greet_served)

    def count(flag):
        return flag.astype(jnp.int32)

    pl.semaphore_wait(
        bar,
        2 * ny - 1 + count(has_low) + count(has_high) + 2 * (ny - 1) * (count(up) + count(down)) + 2 * count(passes),
    )

    def cross(head):
        for i in range(ny):
            yy = there(i)
            target = (other * ny + yy, b)
            for n, (src, dst) in enumerate(((q, qb), (g, gb))):
                send(
                    src.at[:, :, cols(yy * lh + head)],
                    dst.at[:, part(side * half, y), cols(head)],
                    sqx.at[n], rqx.at[n, head], target,
                )

    cross(0)
    for i in range(ny):
        yy = there(i)
        for n, (src, dst) in enumerate(((k, kb), (v, vb))):
            a, z = src.at[:, :, wide(yy)], dst.at[pl.ds(2, 2), part(0, y), :]
            if i == 0:
                pltpu.make_async_copy(a, z, rk.at[n, 1]).start()
            else:
                send(a, z, sk.at[n, 1], rk.at[n, 1], (side * ny + yy, b))
    for i in range(ny):
        yy = there(i)
        for n, (src, dst) in enumerate(((q, qb), (g, gb))):
            a, z = src.at[:, :, wide(yy)], dst.at[:, part(side * half, y), :]
            if i == 0:
                pltpu.make_async_copy(a, z, rqo.at[n]).start()
            else:
                send(a, z, sqo.at[n], rqo.at[n], (side * ny + yy, b))
    for head in range(1, FIRST):
        cross(head)
    for n, buf in enumerate((kb, vb)):
        take(buf.at[pl.ds(2, 2)], rk.at[n, 1])
        for delta in (1, -1):
            over(
                delta,
                lambda few, buf=buf: buf.at[pl.ds(2, 2), few, :],
                lambda few, buf=buf, delta=delta: buf.at[pl.ds(2 * (1 - delta), 2), few, :],
                sk.at[n, 1 + delta], rk.at[n, 1 - delta], pkv.at[n], rpk.at[n],
            )
    for head in range(FIRST, AHEAD):
        cross(head)
    mid = pl.ds(pl.multiple_of(passed * rows, 16), rows)

    @pl.when(passes)
    def _():
        for n, buf in enumerate((kb, vb)):
            take(pkv.at[n], rpk.at[n])
            send(pkv.at[n], buf.at[pl.ds(4 * pass_in, 2), mid, :], spk.at[n], rk.at[n, 2 * pass_in], pass_to)

    def pass_on(head):
        c = cols(head)
        for n, buf in enumerate((dkn, dvn)):
            a = pdkv.at[n, :, :, c]
            take(a, rpd.at[n, head])
            send(a, buf.at[pass_in, :, mid, c], spd.at[n], rdn.at[n, pass_in, head], pass_to)

    def clear(at):
        dkn[at] = jnp.zeros(dkn.shape[1:], BF16)
        dvn[at] = jnp.zeros(dvn.shape[1:], BF16)

    pl.when(jnp.logical_not(has_low))(lambda: clear(0))
    pl.when(jnp.logical_not(has_high))(lambda: clear(1))

    for n, buf in enumerate((qb, gb)):
        take(buf.at[:, pl.ds(pl.multiple_of(side * half, 16), half), :], rqo.at[n])
    for delta in (1, -1):

        def arrived(delta=delta):
            for n, buf in enumerate((kb, vb)):
                take(buf.at[pl.ds(2 * (1 + delta), 2)], rk.at[n, 1 + delta])

        near(delta, arrived)

    def slot(t, s):
        return jnp.clip(tp[2 * b + t, s] - 2 * b + 2, 0, 5)

    def merge(l1, r1, l2, r2):
        top = jnp.maximum(l1, l2)
        total = top + jnp.log(jnp.exp(l1 - top) + jnp.exp(l2 - top))
        return total, r1 * jnp.exp(l1 - total) + r2 * jnp.exp(l2 - total)

    def first(head):
        c = cols(head)
        for t in range(2):
            qf, gf = qb[t, :, c], gb[t, :, c]
            log_total = row_dot = None
            for s in range(keep):
                at = slot(t, s)
                scores = dot(kb[at, :, c], qf, 1, 1) * scale
                grad_p = dot(vb[at, :, c], gf, 1, 1)
                top = jnp.max(scores, axis=0, keepdims=True)
                e = jnp.exp(scores - top)
                total = jnp.sum(e, axis=0, keepdims=True)
                weighted = jnp.sum(e * grad_p, axis=0, keepdims=True) / total
                total = top + jnp.log(total)
                if s:
                    log_total, row_dot = merge(log_total, row_dot, total, weighted)
                else:
                    log_total, row_dot = total, weighted
            st_s[head, pl.ds(2 * t, 1), :] = log_total
            st_s[head, pl.ds(2 * t + 1, 1), :] = row_dot
        send(st_s.at[head], st_r.at[head], sst.at[head], rst.at[head], (other * ny + y, b))

    def second(head):
        c = cols(head)
        for t in range(2):
            qf, gf = qb[t, :, c], gb[t, :, c]
            log_total, row_dot = merge(
                st_s[head, pl.ds(2 * t, 1), :], st_s[head, pl.ds(2 * t + 1, 1), :],
                st_r[head, pl.ds(2 * t, 1), :], st_r[head, pl.ds(2 * t + 1, 1), :],
            )
            grad_q = None
            for s in range(keep):
                at = slot(t, s)
                kt = kb[at, :, c]
                probs = jnp.exp(dot(kt, qf, 1, 1) * scale - log_total)
                grad_s = (probs * (dot(vb[at, :, c], gf, 1, 1) - row_dot)).astype(BF16)
                tv[t * keep + s] = dot(probs.astype(BF16), gf, 1, 0)
                tk[t * keep + s] = dot(grad_s, qf, 1, 0)
                term = dot(kt, grad_s, 0, 0)
                grad_q = term if grad_q is None else grad_q + term
            dqs[t, :, c] = (grad_q * scale).T.astype(BF16)
        mine = cols(y * lh + head)
        for i in range(ny):
            yy = there(i)
            send(dqs.at[:, part(other * half, yy), c], dqx.at[:, :, mine], sdq.at[1], rdq.at[1], (other * ny + yy, b))
        for i in range(ny):
            yy = there(i)
            a, z = dqs.at[:, part(side * half, yy), c], dqo.at[:, :, mine]
            if i == 0:
                pltpu.make_async_copy(a, z, rdq.at[0]).start()
            else:
                send(a, z, sdq.at[0], rdq.at[0], (side * ny + yy, b))
        slots = [slot(t, s) for t in range(2) for s in range(keep)]
        for j in range(6):
            for terms, out, own, factor in ((tk, dks, dko, scale), (tv, dvs, dvo, 1.0)):
                total = None
                for n, at in enumerate(slots):
                    term = jnp.where(at == j, terms[n], 0.0)
                    total = term if total is None else total + term
                total = total * factor
                if j // 2 == 1:
                    own[j - 2, :, c] = total
                else:
                    out[j // 4, j % 2, :, c] = total.astype(BF16)
        for delta in (1, -1):
            to, here = (1 + delta) // 2, (1 - delta) // 2
            for n, (src, dst) in enumerate(((dks, dkn), (dvs, dvn))):
                over(
                    delta,
                    lambda few, src=src, to=to: src.at[to, :, few, c],
                    lambda few, dst=dst, here=here: dst.at[here, :, few, c],
                    sdn.at[n, to], rdn.at[n, here, head], pdkv.at[n, :, :, c], rpd.at[n, head],
                )

    def third(head):
        c, mine = cols(head), cols(y * lh + head)
        for n, (own, near_by, final, out) in enumerate(((dko, dkn, dkf, ok), (dvo, dvn, dvf, ov))):
            for here, delta in ((0, -1), (1, 1)):
                near(delta, lambda n=n, buf=near_by, here=here: take(buf.at[here, :, :, c], rdn.at[n, here, head]))
            for t in range(2):
                total = own[t, :, c] + near_by[0, t, :, c].astype(F32) + near_by[1, t, :, c].astype(F32)
                final[t, :, c] = total.astype(BF16)
            for i in range(ny):
                yy = there(i)
                a, z = final.at[:, part(0, yy), c], out.at[:, :, mine]
                if i == 0:
                    pltpu.make_async_copy(a, z, rdk.at[n]).start()
                else:
                    send(a, z, sdk.at[n], rdk.at[n], (side * ny + yy, b))

    def step(at, carry):
        @pl.when(at < lh)
        def _():
            for n, buf in enumerate((qb, gb)):
                take(buf.at[:, pl.ds(pl.multiple_of(other * half, 16), half), cols(at)], rqx.at[n, at])
            pl.when(at + AHEAD < lh)(lambda: cross(at + AHEAD))
            first(at)

        @pl.when(jnp.logical_and(at >= LAG, at < lh + LAG))
        def _():
            take(st_r.at[at - LAG], rst.at[at - LAG])
            second(at - LAG)

        pl.when(jnp.logical_and(jnp.logical_and(at > LAG, at <= lh + LAG), passes))(lambda: pass_on(at - LAG - 1))
        pl.when(at >= LAG + 2)(lambda: third(at - LAG - 2))
        return carry

    lax.fori_loop(0, lh + LAG + 2, step, 0)

    most = pl.ds(0, (ny - 1) * width)
    for n, src in enumerate((q, g)):
        take(src.at[:, :, most], sqo.at[n])
        take(src, sqx.at[n])
    for n, src in enumerate((k, v)):
        take(src.at[:, :, most], sk.at[n, 1])
        for delta, parts in ((-1, (dks, dvs)), (1, (dks, dvs))):
            to = (1 + delta) // 2

            def sent(n=n, delta=delta, to=to, buf=(kb, vb)[n], parts=parts[n]):
                take(buf.at[pl.ds(2, 2)], sk.at[n, 1 + delta])
                take(parts.at[to], sdn.at[n, to])

            near(delta, sent)
    for head in range(lh):
        take(st_s.at[head], sst.at[head])

    @pl.when(passes)
    def _():
        for n in range(2):
            take(pkv.at[n], spk.at[n])
            take(pdkv.at[n], spd.at[n])

    for n, out in enumerate((ok, ov)):
        take(out, rdk.at[n])
        take(out.at[:, :, most], sdk.at[n])
    take(dqo, rdq.at[0])
    take(dqx, rdq.at[1])
    oq[...] = (dqo[...].astype(F32) + dqx[...].astype(F32)).astype(BF16)
    take(dqo.at[:, :, most], sdq.at[0])
    take(dqx, sdq.at[1])


def body(q, k, v, g, tile_pairs):
    ny = lax.axis_size("uly") // SIDES
    nb = lax.axis_size("blk")
    tiles, rows, features = q.shape
    lh = features // HD // ny
    width, half, keep = lh * HD, ny * rows, tile_pairs.shape[1]
    passing = pltpu.VMEM((2, tiles, rows, width), BF16)
    dma = pltpu.SemaphoreType.DMA
    out = jax.ShapeDtypeStruct(q.shape, BF16)
    any_space = pl.BlockSpec(memory_space=pl.ANY)
    vmem = pl.BlockSpec(memory_space=pltpu.VMEM)
    full = pltpu.VMEM((tiles, SIDES * half, width), BF16)
    keys = pltpu.VMEM((3 * tiles, half, width), BF16)
    own = pltpu.VMEM((tiles, rows, features), BF16)
    aside = pltpu.VMEM((2, tiles, half, width), BF16)
    mine = pltpu.VMEM((tiles, half, width), BF16)
    total = pltpu.VMEM((tiles, half, width), F32)
    stats = pltpu.VMEM((lh, 2 * tiles, SIDES * half), F32)
    terms = pltpu.VMEM((tiles * keep, half, HD), F32)
    return pl.pallas_call(
        functools.partial(kernel, (ny, nb, lh, rows, keep)),
        out_shape=(out, out, out),
        in_specs=[pl.BlockSpec(memory_space=pltpu.SMEM)] + [any_space] * 4,
        out_specs=(vmem, vmem, vmem),
        scratch_shapes=[
            full, full, keys, keys, stats, stats, full, aside, aside, mine, mine, own, own, aside, aside, total, total,
            terms, terms, passing, passing,
            dma((2,)), dma((2, lh)), dma((2, 3)), dma((lh,)), dma((2,)), dma((2, 2, lh)), dma((2,)),
            dma((2,)), dma((2,)), dma((2, 3)), dma((lh,)), dma((2,)), dma((2, 2)), dma((2,)),
            dma((2,)), dma((2,)), dma((2, lh)), dma((2,)),
        ],
        name="tile_attention_backward",
        compiler_params=pltpu.CompilerParams(collective_id=0, has_side_effects=True, vmem_limit_bytes=50 << 20),
    )(tile_pairs, q, k, v, g)


def solution(mesh):
    split = P("blk", "uly", None)
    return jax.shard_map(
        body, mesh=mesh, in_specs=(split,) * 4 + (P(),), out_specs=(split,) * 3, check_vma=False
    )
```

```python
import functools
import math

import jax
import jax.numpy as jnp
from jax import lax
from jax.experimental import pallas as pl
from jax.experimental.pallas import tpu as pltpu
from jax.sharding import PartitionSpec as P

HD = 128
MESH = pl.DeviceIdType.MESH
F32 = jnp.float32
BF16 = jnp.bfloat16
SIDES = 2
FIRST = 2
AHEAD = 4
LAG = 4
PLANE = 8


def dot(a, b, ca, cb):
    return lax.dot_general(a, b, (((ca,), (cb,)), ((), ())), preferred_element_type=F32)


def kernel(cfg, tp, q, k, v, g, dqo, dqx, ok, ov, qb, gb, kb, vb, st_s, st_r, dqs, dks, dvs, dkf, dvf, dkn, dvn, dko, dvo, tk, tv, pkv, pdkv,
           rqo, rqx, rk, rst, rdq, rdn, rdk, sqo, sqx, sk, sst, sdq, sdn, sdk, rpk, spk, rpd, spd, pace):
    ny, nb, lh, rows, keep = cfg
    half = ny * rows
    width = lh * HD
    scale = 1.0 / math.sqrt(HD)
    u, b = lax.axis_index("uly"), lax.axis_index("blk")
    side, y = u // ny, lax.rem(u, ny)
    other = 1 - side
    has_low, has_high = b > 0, b < nb - 1
    plane, place = b // PLANE, lax.rem(b, PLANE)
    upward = lax.rem(place, 2)
    passed = (place + upward) // 2
    passes = jnp.where(
        upward == 1,
        jnp.logical_and(place < PLANE - 1, plane < nb // PLANE - 1),
        jnp.logical_and(place > 0, plane > 0),
    )
    pass_from = PLANE * plane + (PLANE - 1) * upward
    pass_to = (u, pass_from + 2 * upward - 1)
    pass_in = 1 - upward

    def at_edge(delta):
        return place == (PLANE - 1 if delta > 0 else 0)

    def helper(delta, i):
        return (u, PLANE * plane + (2 * i - 1 if delta > 0 else 2 * i))

    def there(i):
        return lax.rem(y + i, ny)

    def near(delta, action):
        if delta == 0:
            action()
        elif delta < 0:
            pl.when(has_low)(action)
        else:
            pl.when(has_high)(action)

    def cols(head):
        return pl.ds(pl.multiple_of(head * HD, HD), HD)

    def wide(yy):
        return pl.ds(pl.multiple_of(yy * width, HD), width)

    def part(base, yy):
        return pl.ds(pl.multiple_of(base + yy * rows, 16), rows)

    def send(src, dst, ssem, rsem, target):
        pltpu.make_async_remote_copy(
            src_ref=src, dst_ref=dst, send_sem=ssem, recv_sem=rsem, device_id=target, device_id_type=MESH
        ).start()

    def take(ref, sem):
        pltpu.make_async_copy(ref, ref, sem).wait()

    def over(delta, src, dst, ssem, rsem, passing, psem):
        def action():
            @pl.when(at_edge(delta))
            def _():
                for i in range(ny):
                    few = pl.ds(i * rows, rows)
                    if i:
                        send(src(few), passing, ssem, psem, helper(delta, i))
                    else:
                        send(src(few), dst(few), ssem, rsem, (u, b + delta))

            @pl.when(jnp.logical_not(at_edge(delta)))
            def _():
                every = pl.ds(0, half)
                send(src(every), dst(every), ssem, rsem, (u, b + delta))

        near(delta, action)

    bar = pltpu.get_barrier_semaphore()

    def greet(target):
        pl.semaphore_signal(bar, inc=1, device_id=target, device_id_type=MESH)

    for i in range(ny):
        if i:
            greet((side * ny + there(i), b))
        greet((other * ny + there(i), b))

    near(-1, lambda: greet((u, b - 1)))
    near(1, lambda: greet((u, b + 1)))

    def greet_helpers(delta):
        for i in range(1, ny):
            greet(helper(delta, i))
            greet((u, PLANE * (plane + delta) + (2 * i if delta > 0 else 2 * i - 1)))

    def greet_served():
        greet((u, pass_from))
        greet(pass_to)

    up, down = jnp.logical_and(has_high, at_edge(1)), jnp.logical_and(has_low, at_edge(-1))
    pl.when(up)(lambda: greet_helpers(1))
    pl.when(down)(lambda: greet_helpers(-1))
    pl.when(passes)(greet_served)

    planes = nb // PLANE
    z = side * planes + plane

    def along(dz, dc):
        zz = lax.rem(z + dz + 2 * planes, 2 * planes)
        return (zz // planes * ny + y, lax.rem(zz, planes) * PLANE + place + dc * (1 - 2 * lax.rem(place, 2)))

    partners = [along(1, 0), along(-1, 0), along(0, 1)]
    for partner in partners:
        greet(partner)

    def count(flag):
        return flag.astype(jnp.int32)

    pl.semaphore_wait(
        bar,
        2 * ny - 1 + len(partners) + count(has_low) + count(has_high) + 2 * (ny - 1) * (count(up) + count(down)) + 2 * count(passes),
    )

    def cross(head):
        for i in range(ny):
            yy = there(i)
            target = (other * ny + yy, b)
            for n, (src, dst) in enumerate(((q, qb), (g, gb))):
                send(
                    src.at[:, :, cols(yy * lh + head)],
                    dst.at[:, part(side * half, y), cols(head)],
                    sqx.at[n], rqx.at[n, head], target,
                )

    cross(0)
    for i in range(ny):
        yy = there(i)
        for n, (src, dst) in enumerate(((k, kb), (v, vb))):
            a, z = src.at[:, :, wide(yy)], dst.at[pl.ds(2, 2), part(0, y), :]
            if i == 0:
                pltpu.make_async_copy(a, z, rk.at[n, 1]).start()
            else:
                send(a, z, sk.at[n, 1], rk.at[n, 1], (side * ny + yy, b))
    for i in range(ny):
        yy = there(i)
        for n, (src, dst) in enumerate(((q, qb), (g, gb))):
            a, z = src.at[:, :, wide(yy)], dst.at[:, part(side * half, y), :]
            if i == 0:
                pltpu.make_async_copy(a, z, rqo.at[n]).start()
            else:
                send(a, z, sqo.at[n], rqo.at[n], (side * ny + yy, b))
    for head in range(1, FIRST):
        cross(head)
    for n, buf in enumerate((kb, vb)):
        take(buf.at[pl.ds(2, 2)], rk.at[n, 1])
        for delta in (1, -1):
            over(
                delta,
                lambda few, buf=buf: buf.at[pl.ds(2, 2), few, :],
                lambda few, buf=buf, delta=delta: buf.at[pl.ds(2 * (1 - delta), 2), few, :],
                sk.at[n, 1 + delta], rk.at[n, 1 - delta], pkv.at[n], rpk.at[n],
            )
    for head in range(FIRST, AHEAD):
        cross(head)
    mid = pl.ds(pl.multiple_of(passed * rows, 16), rows)

    @pl.when(passes)
    def _():
        for n, buf in enumerate((kb, vb)):
            take(pkv.at[n], rpk.at[n])
            send(pkv.at[n], buf.at[pl.ds(4 * pass_in, 2), mid, :], spk.at[n], rk.at[n, 2 * pass_in], pass_to)

    def pass_on(head):
        c = cols(head)
        for n, buf in enumerate((dkn, dvn)):
            a = pdkv.at[n, :, :, c]
            take(a, rpd.at[n, head])
            send(a, buf.at[pass_in, :, mid, c], spd.at[n], rdn.at[n, pass_in, head], pass_to)

    def clear(at):
        dkn[at] = jnp.zeros(dkn.shape[1:], BF16)
        dvn[at] = jnp.zeros(dvn.shape[1:], BF16)

    pl.when(jnp.logical_not(has_low))(lambda: clear(0))
    pl.when(jnp.logical_not(has_high))(lambda: clear(1))

    for n, buf in enumerate((qb, gb)):
        take(buf.at[:, pl.ds(pl.multiple_of(side * half, 16), half), :], rqo.at[n])
    for delta in (1, -1):

        def arrived(delta=delta):
            for n, buf in enumerate((kb, vb)):
                take(buf.at[pl.ds(2 * (1 + delta), 2)], rk.at[n, 1 + delta])

        near(delta, arrived)

    def slot(t, s):
        return jnp.clip(tp[2 * b + t, s] - 2 * b + 2, 0, 5)

    def merge(l1, r1, l2, r2):
        top = jnp.maximum(l1, l2)
        total = top + jnp.log(jnp.exp(l1 - top) + jnp.exp(l2 - top))
        return total, r1 * jnp.exp(l1 - total) + r2 * jnp.exp(l2 - total)

    def first(head):
        c = cols(head)
        for t in range(2):
            qf, gf = qb[t, :, c], gb[t, :, c]
            log_total = row_dot = None
            for s in range(keep):
                at = slot(t, s)
                scores = dot(kb[at, :, c], qf, 1, 1) * scale
                grad_p = dot(vb[at, :, c], gf, 1, 1)
                top = jnp.max(scores, axis=0, keepdims=True)
                e = jnp.exp(scores - top)
                total = jnp.sum(e, axis=0, keepdims=True)
                weighted = jnp.sum(e * grad_p, axis=0, keepdims=True) / total
                total = top + jnp.log(total)
                if s:
                    log_total, row_dot = merge(log_total, row_dot, total, weighted)
                else:
                    log_total, row_dot = total, weighted
            st_s[head, pl.ds(2 * t, 1), :] = log_total
            st_s[head, pl.ds(2 * t + 1, 1), :] = row_dot
        send(st_s.at[head], st_r.at[head], sst.at[head], rst.at[head], (other * ny + y, b))

    def second(head):
        c = cols(head)
        for t in range(2):
            qf, gf = qb[t, :, c], gb[t, :, c]
            log_total, row_dot = merge(
                st_s[head, pl.ds(2 * t, 1), :], st_s[head, pl.ds(2 * t + 1, 1), :],
                st_r[head, pl.ds(2 * t, 1), :], st_r[head, pl.ds(2 * t + 1, 1), :],
            )
            grad_q = None
            for s in range(keep):
                at = slot(t, s)
                kt = kb[at, :, c]
                probs = jnp.exp(dot(kt, qf, 1, 1) * scale - log_total)
                grad_s = (probs * (dot(vb[at, :, c], gf, 1, 1) - row_dot)).astype(BF16)
                tv[t * keep + s] = dot(probs.astype(BF16), gf, 1, 0)
                tk[t * keep + s] = dot(grad_s, qf, 1, 0)
                term = dot(kt, grad_s, 0, 0)
                grad_q = term if grad_q is None else grad_q + term
            dqs[t, :, c] = (grad_q * scale).T.astype(BF16)
        mine = cols(y * lh + head)
        for i in range(ny):
            yy = there(i)
            send(dqs.at[:, part(other * half, yy), c], dqx.at[:, :, mine], sdq.at[1], rdq.at[1], (other * ny + yy, b))
        for i in range(ny):
            yy = there(i)
            a, z = dqs.at[:, part(side * half, yy), c], dqo.at[:, :, mine]
            if i == 0:
                pltpu.make_async_copy(a, z, rdq.at[0]).start()
            else:
                send(a, z, sdq.at[0], rdq.at[0], (side * ny + yy, b))
        slots = [slot(t, s) for t in range(2) for s in range(keep)]
        for j in range(6):
            for terms, out, own, factor in ((tk, dks, dko, scale), (tv, dvs, dvo, 1.0)):
                total = None
                for n, at in enumerate(slots):
                    term = jnp.where(at == j, terms[n], 0.0)
                    total = term if total is None else total + term
                total = total * factor
                if j // 2 == 1:
                    own[j - 2, :, c] = total
                else:
                    out[j // 4, j % 2, :, c] = total.astype(BF16)
        for delta in (1, -1):
            to, here = (1 + delta) // 2, (1 - delta) // 2
            for n, (src, dst) in enumerate(((dks, dkn), (dvs, dvn))):
                over(
                    delta,
                    lambda few, src=src, to=to: src.at[to, :, few, c],
                    lambda few, dst=dst, here=here: dst.at[here, :, few, c],
                    sdn.at[n, to], rdn.at[n, here, head], pdkv.at[n, :, :, c], rpd.at[n, head],
                )

    def third(head):
        c, mine = cols(head), cols(y * lh + head)
        for n, (own, near_by, final, out) in enumerate(((dko, dkn, dkf, ok), (dvo, dvn, dvf, ov))):
            for here, delta in ((0, -1), (1, 1)):
                near(delta, lambda n=n, buf=near_by, here=here: take(buf.at[here, :, :, c], rdn.at[n, here, head]))
            for t in range(2):
                total = own[t, :, c] + near_by[0, t, :, c].astype(F32) + near_by[1, t, :, c].astype(F32)
                final[t, :, c] = total.astype(BF16)
            for i in range(ny):
                yy = there(i)
                a, z = final.at[:, part(0, yy), c], out.at[:, :, mine]
                if i == 0:
                    pltpu.make_async_copy(a, z, rdk.at[n]).start()
                else:
                    send(a, z, sdk.at[n], rdk.at[n], (side * ny + yy, b))

    def step(at, carry):
        @pl.when(jnp.logical_and(at >= 1, at < lh + 1))
        def _():
            for n in range(len(partners)):
                pl.semaphore_wait(pace.at[n], 1)

        @pl.when(at < lh)
        def _():
            for n, buf in enumerate((qb, gb)):
                take(buf.at[:, pl.ds(pl.multiple_of(other * half, 16), half), cols(at)], rqx.at[n, at])
            for n, partner in zip((1, 0, 2), partners):
                pl.semaphore_signal(pace.at[n], inc=1, device_id=partner, device_id_type=MESH)
            pl.when(at + AHEAD < lh)(lambda: cross(at + AHEAD))
            first(at)

        @pl.when(jnp.logical_and(at >= LAG, at < lh + LAG))
        def _():
            take(st_r.at[at - LAG], rst.at[at - LAG])
            second(at - LAG)

        pl.when(jnp.logical_and(jnp.logical_and(at > LAG, at <= lh + LAG), passes))(lambda: pass_on(at - LAG - 1))
        pl.when(at >= LAG + 2)(lambda: third(at - LAG - 2))
        return carry

    lax.fori_loop(0, lh + LAG + 2, step, 0)

    most = pl.ds(0, (ny - 1) * width)
    for n, src in enumerate((q, g)):
        take(src.at[:, :, most], sqo.at[n])
        take(src, sqx.at[n])
    for n, src in enumerate((k, v)):
        take(src.at[:, :, most], sk.at[n, 1])
        for delta, parts in ((-1, (dks, dvs)), (1, (dks, dvs))):
            to = (1 + delta) // 2

            def sent(n=n, delta=delta, to=to, buf=(kb, vb)[n], parts=parts[n]):
                take(buf.at[pl.ds(2, 2)], sk.at[n, 1 + delta])
                take(parts.at[to], sdn.at[n, to])

            near(delta, sent)
    for head in range(lh):
        take(st_s.at[head], sst.at[head])

    @pl.when(passes)
    def _():
        for n in range(2):
            take(pkv.at[n], spk.at[n])
            take(pdkv.at[n], spd.at[n])

    for n, out in enumerate((ok, ov)):
        take(out, rdk.at[n])
        take(out.at[:, :, most], sdk.at[n])
    take(dqo, rdq.at[0])
    take(dqx, rdq.at[1])
    take(dqo.at[:, :, most], sdq.at[0])
    take(dqx, sdq.at[1])


def finish(dqo, dqx, dk, dv, oq, ok, ov, total, sems):
    copies = [pltpu.make_async_copy(a, z, sems.at[n]) for n, (a, z) in enumerate(((dk, ok), (dv, ov), (total, oq)))]
    copies[0].start()
    copies[1].start()
    total[...] = (dqo[...].astype(F32) + dqx[...].astype(F32)).astype(BF16)
    copies[2].start()
    for copy in copies:
        copy.wait()


def body(q, k, v, g, tile_pairs):
    ny = lax.axis_size("uly") // SIDES
    nb = lax.axis_size("blk")
    tiles, rows, features = q.shape
    lh = features // HD // ny
    width, half, keep = lh * HD, ny * rows, tile_pairs.shape[1]
    passing = pltpu.VMEM((2, tiles, rows, width), BF16)
    dma = pltpu.SemaphoreType.DMA
    out = jax.ShapeDtypeStruct(q.shape, BF16)
    any_space = pl.BlockSpec(memory_space=pl.ANY)
    vmem = pl.BlockSpec(memory_space=pltpu.VMEM)
    full = pltpu.VMEM((tiles, SIDES * half, width), BF16)
    keys = pltpu.VMEM((3 * tiles, half, width), BF16)
    aside = pltpu.VMEM((2, tiles, half, width), BF16)
    mine = pltpu.VMEM((tiles, half, width), BF16)
    total = pltpu.VMEM((tiles, half, width), F32)
    stats = pltpu.VMEM((lh, 2 * tiles, SIDES * half), F32)
    terms = pltpu.VMEM((tiles * keep, half, HD), F32)
    results = pl.pallas_call(
        functools.partial(kernel, (ny, nb, lh, rows, keep)),
        out_shape=(out,) * 4,
        in_specs=[pl.BlockSpec(memory_space=pltpu.SMEM)] + [any_space] * 4,
        out_specs=(vmem,) * 4,
        scratch_shapes=[
            full, full, keys, keys, stats, stats, full, aside, aside, mine, mine, aside, aside, total, total,
            terms, terms, passing, passing,
            dma((2,)), dma((2, lh)), dma((2, 3)), dma((lh,)), dma((2,)), dma((2, 2, lh)), dma((2,)),
            dma((2,)), dma((2,)), dma((2, 3)), dma((lh,)), dma((2,)), dma((2, 2)), dma((2,)),
            dma((2,)), dma((2,)), dma((2, lh)), dma((2,)), pltpu.SemaphoreType.REGULAR((3,)),
        ],
        name="tile_attention_backward",
        compiler_params=pltpu.CompilerParams(collective_id=0, has_side_effects=True, vmem_limit_bytes=51 << 20),
    )(tile_pairs, q, k, v, g)
    return pl.pallas_call(
        finish,
        out_shape=(out,) * 3,
        in_specs=[vmem] * 4,
        out_specs=(any_space,) * 3,
        scratch_shapes=[pltpu.VMEM(q.shape, BF16), dma((3,))],
        name="finish",
        compiler_params=pltpu.CompilerParams(vmem_limit_bytes=8 << 20),
    )(*results)


def solution(mesh):
    split = P("blk", "uly", None)
    return jax.shard_map(
        body, mesh=mesh, in_specs=(split,) * 4 + (P(),), out_specs=(split,) * 3, check_vma=False
    )
```

```python
import functools
import math

import jax
import jax.numpy as jnp
from jax import lax
from jax.experimental import pallas as pl
from jax.experimental.pallas import tpu as pltpu
from jax.sharding import PartitionSpec as P

HD = 128
MESH = pl.DeviceIdType.MESH
F32 = jnp.float32
BF16 = jnp.bfloat16
SIDES = 2
FIRST = 2
AHEAD = 4
LAG = 4
PLANE = 8


def dot(a, b, ca, cb):
    return lax.dot_general(a, b, (((ca,), (cb,)), ((), ())), preferred_element_type=F32)


def kernel(cfg, tp, q, k, v, g, dqo, dqx, ok, ov, qb, gb, kb, vb, st_s, st_r, dqs, dks, dvs, dkf, dvf, dkn, dvn, dko, dvo, tk, tv, pkv, pdkv,
           rqo, rqx, rk, rst, rdq, rdn, rdk, sqo, sqx, sk, sst, sdq, sdn, sdk, rpk, spk, rpd, spd):
    ny, nb, lh, rows, keep = cfg
    half = ny * rows
    width = lh * HD
    scale = 1.0 / math.sqrt(HD)
    u, b = lax.axis_index("uly"), lax.axis_index("blk")
    side, y = u // ny, lax.rem(u, ny)
    other = 1 - side
    has_low, has_high = b > 0, b < nb - 1
    plane, place = b // PLANE, lax.rem(b, PLANE)
    upward = lax.rem(place, 2)
    passed = (place + upward) // 2
    passes = jnp.where(
        upward == 1,
        jnp.logical_and(place < PLANE - 1, plane < nb // PLANE - 1),
        jnp.logical_and(place > 0, plane > 0),
    )
    pass_from = PLANE * plane + (PLANE - 1) * upward
    pass_to = (u, pass_from + 2 * upward - 1)
    pass_in = 1 - upward

    def at_edge(delta):
        return place == (PLANE - 1 if delta > 0 else 0)

    def helper(delta, i):
        return (u, PLANE * plane + (2 * i - 1 if delta > 0 else 2 * i))

    def there(i):
        return lax.rem(y + i, ny)

    def near(delta, action):
        if delta == 0:
            action()
        elif delta < 0:
            pl.when(has_low)(action)
        else:
            pl.when(has_high)(action)

    def cols(head):
        return pl.ds(pl.multiple_of(head * HD, HD), HD)

    def wide(yy):
        return pl.ds(pl.multiple_of(yy * width, HD), width)

    def part(base, yy):
        return pl.ds(pl.multiple_of(base + yy * rows, 16), rows)

    def send(src, dst, ssem, rsem, target):
        pltpu.make_async_remote_copy(
            src_ref=src, dst_ref=dst, send_sem=ssem, recv_sem=rsem, device_id=target, device_id_type=MESH
        ).start()

    def take(ref, sem):
        pltpu.make_async_copy(ref, ref, sem).wait()

    def over(delta, src, dst, ssem, rsem, passing, psem):
        def action():
            @pl.when(at_edge(delta))
            def _():
                for i in range(ny):
                    few = pl.ds(i * rows, rows)
                    if i:
                        send(src(few), passing, ssem, psem, helper(delta, i))
                    else:
                        send(src(few), dst(few), ssem, rsem, (u, b + delta))

            @pl.when(jnp.logical_not(at_edge(delta)))
            def _():
                every = pl.ds(0, half)
                send(src(every), dst(every), ssem, rsem, (u, b + delta))

        near(delta, action)

    bar = pltpu.get_barrier_semaphore()

    def greet(target):
        pl.semaphore_signal(bar, inc=1, device_id=target, device_id_type=MESH)

    for i in range(ny):
        if i:
            greet((side * ny + there(i), b))
        greet((other * ny + there(i), b))

    near(-1, lambda: greet((u, b - 1)))
    near(1, lambda: greet((u, b + 1)))

    def greet_helpers(delta):
        for i in range(1, ny):
            greet(helper(delta, i))
            greet((u, PLANE * (plane + delta) + (2 * i if delta > 0 else 2 * i - 1)))

    def greet_served():
        greet((u, pass_from))
        greet(pass_to)

    up, down = jnp.logical_and(has_high, at_edge(1)), jnp.logical_and(has_low, at_edge(-1))
    pl.when(up)(lambda: greet_helpers(1))
    pl.when(down)(lambda: greet_helpers(-1))
    pl.when(passes)(greet_served)

    def count(flag):
        return flag.astype(jnp.int32)

    pl.semaphore_wait(
        bar,
        2 * ny - 1 + count(has_low) + count(has_high) + 2 * (ny - 1) * (count(up) + count(down)) + 2 * count(passes),
    )

    def cross(head):
        for i in range(ny):
            yy = there(i)
            target = (other * ny + yy, b)
            for n, (src, dst) in enumerate(((q, qb), (g, gb))):
                send(
                    src.at[:, :, cols(yy * lh + head)],
                    dst.at[:, part(side * half, y), cols(head)],
                    sqx.at[n], rqx.at[n, head], target,
                )

    cross(0)
    for i in range(ny):
        yy = there(i)
        for n, (src, dst) in enumerate(((k, kb), (v, vb))):
            a, z = src.at[:, :, wide(yy)], dst.at[pl.ds(2, 2), part(0, y), :]
            if i == 0:
                pltpu.make_async_copy(a, z, rk.at[n, 1]).start()
            else:
                send(a, z, sk.at[n, 1], rk.at[n, 1], (side * ny + yy, b))
    for i in range(ny):
        yy = there(i)
        for n, (src, dst) in enumerate(((q, qb), (g, gb))):
            a, z = src.at[:, :, wide(yy)], dst.at[:, part(side * half, y), :]
            if i == 0:
                pltpu.make_async_copy(a, z, rqo.at[n]).start()
            else:
                send(a, z, sqo.at[n], rqo.at[n], (side * ny + yy, b))
    for head in range(1, FIRST):
        cross(head)
    for n, buf in enumerate((kb, vb)):
        take(buf.at[pl.ds(2, 2)], rk.at[n, 1])
        for delta in (1, -1):
            over(
                delta,
                lambda few, buf=buf: buf.at[pl.ds(2, 2), few, :],
                lambda few, buf=buf, delta=delta: buf.at[pl.ds(2 * (1 - delta), 2), few, :],
                sk.at[n, 1 + delta], rk.at[n, 1 - delta], pkv.at[n], rpk.at[n],
            )
    for head in range(FIRST, AHEAD):
        cross(head)
    mid = pl.ds(pl.multiple_of(passed * rows, 16), rows)

    @pl.when(passes)
    def _():
        for n, buf in enumerate((kb, vb)):
            take(pkv.at[n], rpk.at[n])
            send(pkv.at[n], buf.at[pl.ds(4 * pass_in, 2), mid, :], spk.at[n], rk.at[n, 2 * pass_in], pass_to)

    def pass_on(head):
        c = cols(head)
        for n, buf in enumerate((dkn, dvn)):
            a = pdkv.at[n, :, :, c]
            take(a, rpd.at[n, head])
            send(a, buf.at[pass_in, :, mid, c], spd.at[n], rdn.at[n, pass_in, head], pass_to)

    def clear(at):
        dkn[at] = jnp.zeros(dkn.shape[1:], BF16)
        dvn[at] = jnp.zeros(dvn.shape[1:], BF16)

    pl.when(jnp.logical_not(has_low))(lambda: clear(0))
    pl.when(jnp.logical_not(has_high))(lambda: clear(1))

    for n, buf in enumerate((qb, gb)):
        take(buf.at[:, pl.ds(pl.multiple_of(side * half, 16), half), :], rqo.at[n])
    for delta in (1, -1):

        def arrived(delta=delta):
            for n, buf in enumerate((kb, vb)):
                take(buf.at[pl.ds(2 * (1 + delta), 2)], rk.at[n, 1 + delta])

        near(delta, arrived)

    def slot(t, s):
        return jnp.clip(tp[2 * b + t, s] - 2 * b + 2, 0, 5)

    def merge(l1, r1, l2, r2):
        top = jnp.maximum(l1, l2)
        total = top + jnp.log(jnp.exp(l1 - top) + jnp.exp(l2 - top))
        return total, r1 * jnp.exp(l1 - total) + r2 * jnp.exp(l2 - total)

    def first(head):
        c = cols(head)
        for t in range(2):
            qf, gf = qb[t, :, c], gb[t, :, c]
            log_total = row_dot = None
            for s in range(keep):
                at = slot(t, s)
                scores = dot(kb[at, :, c], qf, 1, 1) * scale
                grad_p = dot(vb[at, :, c], gf, 1, 1)
                top = jnp.max(scores, axis=0, keepdims=True)
                e = jnp.exp(scores - top)
                total = jnp.sum(e, axis=0, keepdims=True)
                weighted = jnp.sum(e * grad_p, axis=0, keepdims=True) / total
                total = top + jnp.log(total)
                if s:
                    log_total, row_dot = merge(log_total, row_dot, total, weighted)
                else:
                    log_total, row_dot = total, weighted
            st_s[head, pl.ds(2 * t, 1), :] = log_total
            st_s[head, pl.ds(2 * t + 1, 1), :] = row_dot
        send(st_s.at[head], st_r.at[head], sst.at[head], rst.at[head], (other * ny + y, b))

    def second(head):
        c = cols(head)
        for t in range(2):
            qf, gf = qb[t, :, c], gb[t, :, c]
            log_total, row_dot = merge(
                st_s[head, pl.ds(2 * t, 1), :], st_s[head, pl.ds(2 * t + 1, 1), :],
                st_r[head, pl.ds(2 * t, 1), :], st_r[head, pl.ds(2 * t + 1, 1), :],
            )
            grad_q = None
            for s in range(keep):
                at = slot(t, s)
                kt = kb[at, :, c]
                probs = jnp.exp(dot(kt, qf, 1, 1) * scale - log_total)
                grad_s = (probs * (dot(vb[at, :, c], gf, 1, 1) - row_dot)).astype(BF16)
                tv[t * keep + s] = dot(probs.astype(BF16), gf, 1, 0)
                tk[t * keep + s] = dot(grad_s, qf, 1, 0)
                term = dot(kt, grad_s, 0, 0)
                grad_q = term if grad_q is None else grad_q + term
            dqs[t, :, c] = (grad_q * scale).T.astype(BF16)
        mine = cols(y * lh + head)
        for i in range(ny):
            yy = there(i)
            send(dqs.at[:, part(other * half, yy), c], dqx.at[:, :, mine], sdq.at[1], rdq.at[1], (other * ny + yy, b))
        for i in range(ny):
            yy = there(i)
            a, z = dqs.at[:, part(side * half, yy), c], dqo.at[:, :, mine]
            if i == 0:
                pltpu.make_async_copy(a, z, rdq.at[0]).start()
            else:
                send(a, z, sdq.at[0], rdq.at[0], (side * ny + yy, b))
        slots = [slot(t, s) for t in range(2) for s in range(keep)]
        for j in range(6):
            for terms, out, own, factor in ((tk, dks, dko, scale), (tv, dvs, dvo, 1.0)):
                total = None
                for n, at in enumerate(slots):
                    term = jnp.where(at == j, terms[n], 0.0)
                    total = term if total is None else total + term
                total = total * factor
                if j // 2 == 1:
                    own[j - 2, :, c] = total
                else:
                    out[j // 4, j % 2, :, c] = total.astype(BF16)
        for delta in (1, -1):
            to, here = (1 + delta) // 2, (1 - delta) // 2
            for n, (src, dst) in enumerate(((dks, dkn), (dvs, dvn))):
                over(
                    delta,
                    lambda few, src=src, to=to: src.at[to, :, few, c],
                    lambda few, dst=dst, here=here: dst.at[here, :, few, c],
                    sdn.at[n, to], rdn.at[n, here, head], pdkv.at[n, :, :, c], rpd.at[n, head],
                )

    def third(head):
        c, mine = cols(head), cols(y * lh + head)
        for n, (own, near_by, final, out) in enumerate(((dko, dkn, dkf, ok), (dvo, dvn, dvf, ov))):
            for here, delta in ((0, -1), (1, 1)):
                near(delta, lambda n=n, buf=near_by, here=here: take(buf.at[here, :, :, c], rdn.at[n, here, head]))
            for t in range(2):
                total = own[t, :, c] + near_by[0, t, :, c].astype(F32) + near_by[1, t, :, c].astype(F32)
                final[t, :, c] = total.astype(BF16)
            for i in range(ny):
                yy = there(i)
                a, z = final.at[:, part(0, yy), c], out.at[:, :, mine]
                if i == 0:
                    pltpu.make_async_copy(a, z, rdk.at[n]).start()
                else:
                    send(a, z, sdk.at[n], rdk.at[n], (side * ny + yy, b))

    def step(at, carry):
        @pl.when(at < lh)
        def _():
            for n, buf in enumerate((qb, gb)):
                take(buf.at[:, pl.ds(pl.multiple_of(other * half, 16), half), cols(at)], rqx.at[n, at])
            pl.when(at + AHEAD < lh)(lambda: cross(at + AHEAD))
            first(at)

        @pl.when(jnp.logical_and(at >= LAG, at < lh + LAG))
        def _():
            take(st_r.at[at - LAG], rst.at[at - LAG])
            second(at - LAG)

        pl.when(jnp.logical_and(jnp.logical_and(at > LAG, at <= lh + LAG), passes))(lambda: pass_on(at - LAG - 1))
        pl.when(at >= LAG + 2)(lambda: third(at - LAG - 2))
        return carry

    lax.fori_loop(0, lh + LAG + 2, step, 0)

    most = pl.ds(0, (ny - 1) * width)
    for n, src in enumerate((q, g)):
        take(src.at[:, :, most], sqo.at[n])
        take(src, sqx.at[n])
    for n, src in enumerate((k, v)):
        take(src.at[:, :, most], sk.at[n, 1])
        for delta, parts in ((-1, (dks, dvs)), (1, (dks, dvs))):
            to = (1 + delta) // 2

            def sent(n=n, delta=delta, to=to, buf=(kb, vb)[n], parts=parts[n]):
                take(buf.at[pl.ds(2, 2)], sk.at[n, 1 + delta])
                take(parts.at[to], sdn.at[n, to])

            near(delta, sent)
    for head in range(lh):
        take(st_s.at[head], sst.at[head])

    @pl.when(passes)
    def _():
        for n in range(2):
            take(pkv.at[n], spk.at[n])
            take(pdkv.at[n], spd.at[n])

    for n, out in enumerate((ok, ov)):
        take(out, rdk.at[n])
        take(out.at[:, :, most], sdk.at[n])
    take(dqo, rdq.at[0])
    take(dqx, rdq.at[1])
    take(dqo.at[:, :, most], sdq.at[0])
    take(dqx, sdq.at[1])


def finish(dqo, dqx, dk, dv, oq, ok, ov, total, sems):
    copies = [pltpu.make_async_copy(a, z, sems.at[n]) for n, (a, z) in enumerate(((dk, ok), (dv, ov), (total, oq)))]
    copies[0].start()
    copies[1].start()
    total[...] = (dqo[...].astype(F32) + dqx[...].astype(F32)).astype(BF16)
    copies[2].start()
    for copy in copies:
        copy.wait()


def body(q, k, v, g, tile_pairs):
    ny = lax.axis_size("uly") // SIDES
    nb = lax.axis_size("blk")
    tiles, rows, features = q.shape
    lh = features // HD // ny
    width, half, keep = lh * HD, ny * rows, tile_pairs.shape[1]
    passing = pltpu.VMEM((2, tiles, rows, width), BF16)
    dma = pltpu.SemaphoreType.DMA
    out = jax.ShapeDtypeStruct(q.shape, BF16)
    any_space = pl.BlockSpec(memory_space=pl.ANY)
    vmem = pl.BlockSpec(memory_space=pltpu.VMEM)
    full = pltpu.VMEM((tiles, SIDES * half, width), BF16)
    keys = pltpu.VMEM((3 * tiles, half, width), BF16)
    aside = pltpu.VMEM((2, tiles, half, width), BF16)
    mine = pltpu.VMEM((tiles, half, width), BF16)
    total = pltpu.VMEM((tiles, half, width), F32)
    stats = pltpu.VMEM((lh, 2 * tiles, SIDES * half), F32)
    terms = pltpu.VMEM((tiles * keep, half, HD), F32)
    results = pl.pallas_call(
        functools.partial(kernel, (ny, nb, lh, rows, keep)),
        out_shape=(out,) * 4,
        in_specs=[pl.BlockSpec(memory_space=pltpu.SMEM)] + [any_space] * 4,
        out_specs=(vmem,) * 4,
        scratch_shapes=[
            full, full, keys, keys, stats, stats, full, aside, aside, mine, mine, aside, aside, total, total,
            terms, terms, passing, passing,
            dma((2,)), dma((2, lh)), dma((2, 3)), dma((lh,)), dma((2,)), dma((2, 2, lh)), dma((2,)),
            dma((2,)), dma((2,)), dma((2, 3)), dma((lh,)), dma((2,)), dma((2, 2)), dma((2,)),
            dma((2,)), dma((2,)), dma((2, lh)), dma((2,)),
        ],
        name="tile_attention_backward",
        compiler_params=pltpu.CompilerParams(collective_id=0, has_side_effects=True, vmem_limit_bytes=51 << 20),
    )(tile_pairs, q, k, v, g)
    return pl.pallas_call(
        finish,
        out_shape=(out,) * 3,
        in_specs=[vmem] * 4,
        out_specs=(any_space,) * 3,
        scratch_shapes=[pltpu.VMEM(q.shape, BF16), dma((3,))],
        name="finish",
        compiler_params=pltpu.CompilerParams(vmem_limit_bytes=8 << 20),
    )(*results)


def solution(mesh):
    split = P("blk", "uly", None)
    return jax.shard_map(
        body, mesh=mesh, in_specs=(split,) * 4 + (P(),), out_specs=(split,) * 3, check_vma=False
    )
```
